32 devices in a mesh: dp: 8 (over z, core), feat: 4 (over y, x).
Axes of the slice: x: 2, y: 2, z: 4, core: 2. Of those that a mesh axis runs over, the one named last changes fastest.
Arguments:
- bins: int32 [512, 24576], P('feat', 'dp'), may hold values from 0 to 255, as said below
- grads: float32 [8, 24576], P(None, 'dp'), may hold values from -6 to 6
- hess: float32 [8, 24576], P(None, 'dp'), may hold values from 0.05 to 1
- nodes: int32 [24576], P('dp'), may hold values from 0 to 3
- row_count: int32 [8], P('dp'), may hold values from 1 to 3072, 15360 in all
Outputs:
- best_gain: float32 [4, 512], P(None, 'feat')
The draws below stay inside these ranges and needn't reach their ends.
Inputs may be any that keep to these rules, and one draw needn't show every extreme that they name: Row slots at or beyond row_count of their dp index are padding; the counts of all dp indices add up to 5 / 8 of 24576. `bins`: each entry is a bin of its feature.
All inputs are finite; a program needn't handle non-finite values. No bound on the sum of `row_count` on one device may be relied on, other than what follows from the above.
Results may differ from the reference program's by a relative error of at most 0.0016.
Values sent between devices are 32-bit elements; how exact they have to be, the bound alone decides.
A program may use at most 64 MiB of HBM per device.

```python
import math
import jax
import jax.numpy as jnp
import numpy as np
from jax import lax

FEATS = 512
BINS = 256
OUT = 8
NODES = 4
CAP = 3072
ROWS = 24576
N_DP = 8


def draw_bins(key, part):
    weight_key = jax.random.fold_in(key, 11)
    pick_key = jax.random.fold_in(key, 23)
    powers = jax.random.randint(weight_key, (FEATS, BINS), 0, 5, dtype=jnp.int32)
    weights = jnp.left_shift(jnp.ones((FEATS, BINS), jnp.int32), powers)
    running = jnp.cumsum(weights, axis=1).astype(jnp.int32)
    totals = running[:, -1:]
    picks = jax.random.randint(pick_key, (FEATS, ROWS), 0, 1 << 30, dtype=jnp.int32)
    picks = (picks % totals).astype(jnp.int32)

    def locate(table, values):
        return jnp.searchsorted(table, values, side='right').astype(jnp.int32)
    return jax.vmap(locate)(running, picks).astype(jnp.int32)


def place_ends(values, key, least, largest):
    extent = values.shape
    place = [jax.random.randint(jax.random.fold_in(key, axis), (), 0, extent[axis]) for axis in range(len(extent))]
    values = values.at[tuple(place)].set(least)
    longest = extent.index(max(extent))
    place[longest] = (place[longest] + 1) % extent[longest]
    return values.at[tuple(place)].set(largest)


def shard_levels(own_key, dims, shards, low, largest):
    factor_of = 1.0
    for axis_at, blocks in shards:
        draws = jax.random.uniform(jax.random.fold_in(jax.random.fold_in(own_key, 6), axis_at), (blocks,), jnp.float32, low / len(shards), largest / len(shards))
        factor_of = factor_of * jnp.repeat(jnp.exp(draws), dims[axis_at] // blocks).reshape((-1,) + (1,) * (len(dims) - 1 - axis_at))
    return factor_of


def profile(amount, total, reach, lean):
    loads = [(1 << 20) // math.isqrt(standing ** lean) + 1 for standing in range(2, amount + 1)]
    spare, counts = total - reach - (amount - 1), [1] * (amount - 1)
    while spare > 0:
        movable = [i for i in range(amount - 1) if counts[i] < reach]
        pool, budget = sum([loads[i] for i in movable]), spare
        for i in movable:
            extra = min(reach - counts[i], max(1, budget * loads[i] // pool), spare)
            counts[i] = counts[i] + extra
            spare = spare - extra
    return np.array([reach] + counts)


def uneven(key, number_of, total, bound, skew):
    if number_of == 2:
        one = jax.random.randint(key, (), max(1, total - bound), min(bound, total - 1) + 1)
        return jnp.stack([one, total - one])
    lengths = jnp.asarray(profile(number_of, total, bound, skew), jnp.int32)
    couples = (number_of - 1) // 2
    giver, taker = lengths[1:1 + 2 * couples:2], lengths[2:2 + 2 * couples:2]
    room = jnp.minimum(giver - 1, bound - taker)
    shifted = jax.random.randint(jax.random.fold_in(key, 1), (couples,), 0, 1 << 20) % (room + 1)
    lengths = lengths.at[1:1 + 2 * couples:2].set(giver - shifted).at[2:2 + 2 * couples:2].set(taker + shifted)
    return lengths[jax.random.permutation(jax.random.fold_in(key, 2), number_of)]


def noise(own_key, shape, width, most, split=(), kind=jnp.bfloat16):
    factor_of = shard_levels(own_key, shape, split, -0.22, 0.18) if split else 1.0
    result = jax.random.normal(own_key, shape, jnp.float32) * width * factor_of
    return jnp.minimum(jnp.maximum(result, -most), most).astype(kind)


def setup_inputs(seed: int = 0) -> dict:
    key_of = jax.random.split(jax.random.key(seed), 6)
    return {
        "bins": draw_bins(jax.random.fold_in(key_of[5], 71), 0),
        "grads": noise(key_of[1], (OUT, ROWS), 1.0, 6.0, ((1, 8),), jnp.float32),
        "hess": jnp.clip(jnp.exp(math.log(1.0) - 2.9957323 * jax.random.uniform(key_of[2], (OUT, ROWS), jnp.float32) ** shard_levels(key_of[2], (OUT, ROWS), ((1, 8),), -0.2, 0.2)), 0.05, 1.0),
        "nodes": place_ends(jax.random.randint(key_of[3], (ROWS,), 0, NODES), jax.random.fold_in(key_of[3], 1), 0, NODES - 1).astype(jnp.int32),
        "row_count": uneven(key_of[4], N_DP, N_DP * CAP * 5 // 8, CAP, 1).astype(jnp.int32),
    }


def split_score(sums):
    shaped = sums.reshape(sums.shape[:-1] + (NODES, 2, OUT))
    grad_sum = shaped[..., 0, :]
    hess_sum = shaped[..., 1, :]
    return jnp.sum(grad_sum * grad_sum / (hess_sum + 1.0), axis=-1)


def split_gain(left_sums, all_sums):
    return split_score(left_sums) + split_score(all_sums - left_sums) - split_score(all_sums)


def reference(bins, grads, hess, nodes, row_count):
    total_rows = bins.shape[1]
    position = jnp.arange(total_rows, dtype=jnp.int32)
    is_live = (position % CAP) < row_count[position // CAP]
    member = (nodes[:, None] == jnp.arange(NODES, dtype=jnp.int32)[None, :]) & is_live[:, None]
    rounded = jnp.concatenate([grads, hess], axis=0).astype(jnp.bfloat16)
    rounded = lax.optimization_barrier(rounded)
    pair_stats = rounded.astype(jnp.float32).T
    weighted = jnp.where(member[:, :, None], pair_stats[:, None, :], jnp.zeros((), pair_stats.dtype))
    weighted = weighted.reshape(total_rows, NODES * 2 * OUT)

    def per_feature(bin_codes):
        return jax.ops.segment_sum(weighted, bin_codes, num_segments=BINS)

    histogram = lax.map(per_feature, bins)
    left_sums = jnp.cumsum(histogram, axis=1)
    all_sums = left_sums[:, -1:, :]
    split_gains = split_gain(left_sums, all_sums)
    return jnp.max(split_gains, axis=1).T
```

```python
import functools
import math

import jax
import jax.numpy as jnp
from jax import lax
from jax.experimental import pallas as pl
from jax.experimental.pallas import tpu as pltpu
from jax.sharding import PartitionSpec as P

BINS = 256
OUT = 8
NODES = 4
PAIR = 2 * OUT
COLS = NODES * PAIR
HIGH = BINS // 2
LANES = 128
ROW_TILE = 512
STEPS = 1
SEND = ((2, 3, 4, 5, 6, 7), (2, 3, 4, 5, 6, 7))
TAKE = ((0, 1, 2, 3, 4, 5, 6, 7), (0, 1, 2, 3, 4, 5, 6, 7))
OVER_LANES = (((1,), (1,)), ((), ()))
MASK = jnp.float8_e4m3fn


def columns(sums):
    shaped = sums.reshape(NODES, PAIR, sums.shape[-1])
    return shaped[:, :OUT, :], shaped[:, OUT:, :] + 1.0


def score(sums):
    grad_sum, hess_sum = columns(sums)
    return jnp.sum(grad_sum * grad_sum / hess_sum, axis=1)


def two_scores(left, right):
    left_grad, left_hess = columns(left)
    right_grad, right_hess = columns(right)
    top = left_grad * left_grad * right_hess + right_grad * right_grad * left_hess
    return jnp.sum(top / (left_hess * right_hess), axis=1)


def flip(index, k, size):
    other, bit = 0, 1
    while bit < size:
        other = other + ((index // bit + k // bit) % 2) * bit
        bit *= 2
    return other


def kernel(n, bins_ref, grads_ref, hess_ref, nodes_ref, count_ref, out_ref,
           bins_all, stats_all, weights, left_acc, gain_all, labels,
           own_sem, load_sem, bins_send, bins_recv, direct_send, spread_send, core_send, stats_recv,
           gain_send, gain_recv):
    own, rows = bins_all.shape[1:]
    parts = stats_all.shape[1]
    span = rows // parts
    steps, halves = bins_send.shape[1:]
    cut, some_feats = rows // steps, own // halves
    line = n == 8
    near = n // 2
    width = 2 if own % 2 == 0 else 1
    me = lax.axis_index("dp")
    group = lax.axis_index("feat")
    my_part = group % parts
    middle = (me // 2 + me // 4) % 2

    def partner(k):
        return flip(me, k, n)

    def sibling(j):
        return group - my_part + flip(my_part, j, parts)

    def remote(src, dst, send, recv, dp, feat):
        return pltpu.make_async_remote_copy(
            src_ref=src, dst_ref=dst, send_sem=send, recv_sem=recv,
            device_id={"dp": dp, "feat": feat}, device_id_type=pl.DeviceIdType.MESH)

    def bins_copy(k, step, half):
        some = (pl.ds(half * some_feats, some_feats), pl.ds(pl.multiple_of(step * cut, LANES), cut))
        return remote(bins_ref.at[partner(k), *some], bins_all.at[k, *some],
                      bins_send.at[k, step, half], bins_recv.at[k, step, half], partner(k), group)

    def gain_copy(k):
        return remote(gain_all.at[0], gain_all.at[k],
                      gain_send.at[k], gain_recv.at[k], partner(k), group)

    def pair_copy():
        return remote(stats_all.at[0], stats_all.at[1],
                      direct_send.at[1], stats_recv.at[1, 0], partner(1), group)

    def part_copy(k):
        return remote(stats_all.at[0, my_part], stats_all.at[k, my_part],
                      direct_send.at[k], stats_recv.at[k, 0], partner(k), group)

    def spread_copy(k, j):
        return remote(stats_all.at[k, my_part], stats_all.at[k, my_part],
                      spread_send.at[k, j], stats_recv.at[k, j], me, sibling(j))

    def core_copy(k):
        return remote(stats_all.at[k], stats_all.at[k + 1],
                      core_send.at[k], stats_recv.at[k + 1, 0], partner(1), group)

    own_copy = pltpu.make_async_copy(bins_ref.at[me], bins_all.at[0], own_sem)
    loads = [pltpu.make_async_copy(nodes_ref, labels, load_sem.at[0])]
    for part in range(parts):
        some = pl.ds(part * span, span)
        loads.append(pltpu.make_async_copy(
            grads_ref.at[:, some], stats_all.at[0, part, pl.ds(0, OUT), pl.ds(0, span)],
            load_sem.at[1 + 2 * part]))
        loads.append(pltpu.make_async_copy(
            hess_ref.at[:, some], stats_all.at[0, part, pl.ds(OUT, OUT), pl.ds(0, span)],
            load_sem.at[2 + 2 * part]))
    barrier = pltpu.get_barrier_semaphore()

    def greet(dp, feat):
        pl.semaphore_signal(barrier, inc=1, device_id={"dp": dp, "feat": feat},
                            device_id_type=pl.DeviceIdType.MESH)

    @pl.loop(1, n)
    def _(k):
        greet(partner(k), group)

    @pl.loop(1, parts)
    def _(j):
        greet(me, sibling(j))

    for load in loads:
        load.start()
    own_copy.start()
    pl.semaphore_wait(barrier, n - 1 + parts - 1)

    def each_piece(first, last, act, skip=0):
        @pl.loop(first * steps * halves + skip, last * steps * halves)
        def _(at):
            act(bins_copy(at // (steps * halves), at // halves % steps, at % halves))

    def send(copy):
        copy.start()

    loads[0].wait()
    for part in range(parts):
        for row in range(span // LANES):
            at = part * span + row * LANES
            slot_index = at + lax.broadcasted_iota(jnp.int32, (1, LANES), 1)
            stats_all[0, part, row:row + 1, span:] = jnp.where(
                slot_index < count_ref[0], labels[:, at:at + LANES],
                NODES).astype(jnp.float32)
        stats_all[0, part, span // LANES:, span:] = jnp.zeros(
            (PAIR - span // LANES, LANES), jnp.float32)
    for load in loads[1:]:
        load.wait()

    @pl.loop(1, near)
    def _(half):
        part_copy(n - 2 * half).start()

    pair_copy().start()
    each_piece(1, 2, send)
    if line:
        for place in range(2):
            @pl.when(middle == place)
            def _():
                for k in SEND[place]:
                    each_piece(k, k + 1, send)
    else:
        each_piece(2, n, send)

    left_acc[...] = jnp.zeros_like(left_acc)

    def weigh(k):
        for part in range(parts):
            for row in range(span // LANES):
                block = slice(row * LANES, (row + 1) * LANES)
                stats = stats_all[k, part, :, block]
                label = jnp.broadcast_to(
                    stats_all[k, part, row:row + 1, span:], (PAIR, LANES))
                at = part * span + row * LANES
                for node in range(NODES):
                    weights[k, node * PAIR:(node + 1) * PAIR, at:at + LANES] = jnp.where(
                        label == node, stats, 0.0).astype(jnp.bfloat16)

    def add(k, step, half):
        first = half * (some_feats // width)

        @pl.loop(0, some_feats // width, unroll=min(some_feats // width, 4))
        def _(pair):
            at = first + pair
            total = None
            for start in range(0, cut, ROW_TILE):
                size = min(ROW_TILE, cut - start)
                some = pl.ds(pl.multiple_of(step * cut + start, LANES), size)
                whole = weights[k, :, some]
                levels = lax.broadcasted_iota(jnp.int32, (HIGH, size), 0).astype(jnp.int8)
                above, odd = [], [whole]
                for q in range(width):
                    code = bins_all[k, pl.ds(width * at + q, 1), some]
                    high = (code >> 1).astype(jnp.int8)
                    low = (code & 1).astype(jnp.float32).astype(jnp.bfloat16)
                    above.append(jnp.where(
                        jnp.broadcast_to(high, (HIGH, size)) <= levels,
                        jnp.ones((), MASK), jnp.zeros((), MASK)))
                    odd.append(whole * jnp.broadcast_to(low, (COLS, size)))
                part = lax.dot_general(
                    jnp.concatenate(odd, axis=0), jnp.concatenate(above, axis=0),
                    OVER_LANES, preferred_element_type=jnp.float32)
                total = part if total is None else total + part
            for q in range(width):
                mine = slice(q * HIGH, (q + 1) * HIGH)
                feat = width * at + q
                left_acc[feat, :COLS] = left_acc[feat, :COLS] + total[:COLS, mine]
                left_acc[feat, COLS:] = (
                    left_acc[feat, COLS:] + total[(1 + q) * COLS:(2 + q) * COLS, mine])

    def spread(k):
        @pl.loop(1, parts)
        def _(j):
            spread_copy(k, j).start()

    def gather(k):
        @pl.loop(1, parts)
        def _(j):
            spread_copy(k, j).wait_recv()

        core_copy(k).start()

    lane = lax.broadcasted_iota(jnp.int32, (COLS, HIGH), 1)
    wide = gain_all.shape[-1]
    gain_lane = lax.broadcasted_iota(jnp.int32, (NODES, wide), 1)

    def best_of(feat, gains):
        left_odd, odd = left_acc[feat, :COLS], left_acc[feat, COLS:]
        left_even = left_odd - odd + jnp.where(lane == 0, 0.0, pltpu.roll(odd, 1, axis=1))
        total = left_odd[:, HIGH - 1:]
        whole = jnp.broadcast_to(total, (COLS, HIGH))
        gain = jnp.maximum(two_scores(left_even, whole - left_even),
                           two_scores(left_odd, whole - left_odd))
        best = jnp.max(gain, axis=1, keepdims=True) - score(total)
        return jnp.where(gain_lane == me * own + feat,
                         jnp.broadcast_to(best, (NODES, wide)), gains)

    gain_all[0] = jnp.zeros((NODES, wide), jnp.float32)

    def digits(order):
        return sum(k * n ** at for at, k in enumerate(order))

    @pl.loop(0, n)
    def _(turn):
        k = turn
        if line:
            codes = [digits(order) for order in TAKE]
            code = codes[0] + middle * (codes[1] - codes[0])
            for bit in range(3):
                code = code // (1 + (n ** 2 ** bit - 1) * (turn // 2 ** bit % 2))
            k = code % n

        @pl.when(turn == 0)
        def _():
            own_copy.wait()

        @pl.when(turn == 1)
        def _():
            @pl.loop(1, near)
            def _(even):
                part_copy(2 * even).wait_recv()
                spread(2 * even)

            pair_copy().wait_recv()

        @pl.when(turn == 2)
        def _():
            @pl.loop(1, near)
            def _(even):
                gather(2 * even)

            @pl.loop(1, near)
            def _(even):
                core_copy(2 * even).wait_recv()

        weigh(k)

        @pl.loop(0, steps * halves)
        def _(piece):
            step, half = piece // halves, piece % halves

            @pl.when(k > 0)
            def _():
                bins_copy(k, step, half).wait_recv()

            add(k, step, half)

            @pl.when(jnp.logical_and(turn == n - 1, step == steps - 1))
            def _():
                gain_all[0] = lax.fori_loop(0, some_feats, lambda at, gains: best_of(half * some_feats + at, gains),
                                            gain_all[0], unroll=min(some_feats, 4))

    @pl.loop(1, n)
    def _(k):
        gain_copy(n - k).start()

    @pl.loop(1, n)
    def _(k):
        gain_copy(k).wait_recv()

    out_ref[...] = jnp.sum(gain_all[...], axis=0)[:, :out_ref.shape[1]]

    pair_copy().wait_send()
    @pl.loop(1, near)
    def _(half):
        part_copy(2 * half).wait_send()
        core_copy(2 * half).wait_send()

        @pl.loop(1, parts)
        def _(j):
            spread_copy(2 * half, j).wait_send()

    each_piece(1, n, lambda copy: copy.wait_send())

    @pl.loop(1, n)
    def _(k):
        gain_copy(k).wait_send()


def shards(bins, grads, hess, nodes, row_count):
    n = lax.axis_size("dp")
    feats, rows = bins.shape
    own = feats // n
    assert n & (n - 1) == 0 and own * n == feats
    parts = math.gcd(lax.axis_size("feat"), rows // LANES)
    assert n > 7 and parts & (parts - 1) == 0 and rows % (parts * LANES) == 0
    steps = STEPS if rows % (STEPS * LANES) == 0 else 1
    halves = 2 if own % 16 == 0 else 1
    wide = -(-feats // LANES) * LANES
    hbm = pl.BlockSpec(memory_space=pltpu.HBM)
    dma = pltpu.SemaphoreType.DMA
    return pl.pallas_call(
        functools.partial(kernel, n),
        out_shape=jax.ShapeDtypeStruct((NODES, feats), jnp.float32),
        in_specs=[hbm, hbm, hbm, hbm, pl.BlockSpec(memory_space=pltpu.SMEM)],
        out_specs=pl.BlockSpec(memory_space=pltpu.VMEM),
        scratch_shapes=[
            pltpu.VMEM((n, own, rows), jnp.int32),
            pltpu.VMEM((n, parts, PAIR, rows // parts + LANES), jnp.float32),
            pltpu.VMEM((n, COLS, rows), jnp.bfloat16),
            pltpu.VMEM((own, 2 * COLS, HIGH), jnp.float32),
            pltpu.VMEM((n, NODES, wide), jnp.float32),
            pltpu.VMEM((1, rows), jnp.int32),
            dma, dma((1 + 2 * parts,)), dma((n, steps, halves)), dma((n, steps, halves)),
            dma((n,)), dma((n, parts)), dma((n,)), dma((n, parts)),
            dma((n,)), dma((n,)),
        ],
        compiler_params=pltpu.CompilerParams(
            collective_id=0, has_side_effects=True, vmem_limit_bytes=(64 << 20) - 8192),
        name="histogram_gain",
    )(bins.reshape(n, own, rows), grads, hess, nodes.reshape(1, rows), row_count)


def solution(mesh):
    in_specs = (P("feat", "dp"), P(None, "dp"), P(None, "dp"), P("dp"), P("dp"))
    out_specs = P(None, "feat")
    return jax.shard_map(shards, mesh=mesh, in_specs=in_specs, out_specs=out_specs, check_vma=False)
```

```python
import functools
import math

import jax
import jax.numpy as jnp
from jax import lax
from jax.experimental import pallas as pl
from jax.experimental.pallas import tpu as pltpu
from jax.sharding import PartitionSpec as P

BINS = 256
OUT = 8
NODES = 4
PAIR = 2 * OUT
COLS = NODES * PAIR
HIGH = BINS // 2
LANES = 128
ROW_TILE = 512
STEPS = 1
SEND = ((2, 3, 4, 5, 6, 7), (2, 3, 7, 4, 5))
FIRST = 6
TAKE = ((0, 1, 2, 3, 6, 7, 4, 5), (0, 1, 2, 3, 6, 7, 4, 5))
OVER_LANES = (((1,), (1,)), ((), ()))
MASK = jnp.float8_e4m3fn


def columns(sums):
    shaped = sums.reshape(NODES, PAIR, sums.shape[-1])
    return shaped[:, :OUT, :], shaped[:, OUT:, :] + 1.0


def score(sums):
    grad_sum, hess_sum = columns(sums)
    return jnp.sum(grad_sum * grad_sum / hess_sum, axis=1)


def two_scores(left, right):
    left_grad, left_hess = columns(left)
    right_grad, right_hess = columns(right)
    top = left_grad * left_grad * right_hess + right_grad * right_grad * left_hess
    return jnp.sum(top / (left_hess * right_hess), axis=1)


def flip(index, k, size):
    other, bit = 0, 1
    while bit < size:
        other = other + ((index // bit + k // bit) % 2) * bit
        bit *= 2
    return other


def kernel(n, bins_ref, grads_ref, hess_ref, nodes_ref, count_ref, out_ref,
           bins_all, stats_all, weights, left_acc, gain_all, labels,
           own_sem, load_sem, bins_send, bins_recv, direct_send, spread_send, core_send, relay_send, stats_recv,
           gain_send, gain_recv):
    own, rows = bins_all.shape[1:]
    parts = stats_all.shape[1]
    span = rows // parts
    steps, halves = bins_send.shape[1:]
    cut, some_feats = rows // steps, own // halves
    line = n == 8
    near = n // 2
    width = 2 if own % 2 == 0 else 1
    me = lax.axis_index("dp")
    group = lax.axis_index("feat")
    my_part = group % parts
    middle = (me // 2 + me // 4) % 2

    def partner(k):
        return flip(me, k, n)

    def sibling(j):
        return group - my_part + flip(my_part, j, parts)

    def remote(src, dst, send, recv, dp, feat):
        return pltpu.make_async_remote_copy(
            src_ref=src, dst_ref=dst, send_sem=send, recv_sem=recv,
            device_id={"dp": dp, "feat": feat}, device_id_type=pl.DeviceIdType.MESH)

    def bins_copy(k, step, half):
        some = (pl.ds(half * some_feats, some_feats), pl.ds(pl.multiple_of(step * cut, LANES), cut))
        return remote(bins_ref.at[partner(k), *some], bins_all.at[k, *some],
                      bins_send.at[k, step, half], bins_recv.at[k, step, half], partner(k), group)

    def gain_copy(k):
        return remote(gain_all.at[0], gain_all.at[k],
                      gain_send.at[k], gain_recv.at[k], partner(k), group)

    def pair_copy():
        return remote(stats_all.at[0], stats_all.at[1],
                      direct_send.at[1], stats_recv.at[1, 0], partner(1), group)

    def part_copy(k):
        return remote(stats_all.at[0, my_part], stats_all.at[k, my_part],
                      direct_send.at[k], stats_recv.at[k, 0], partner(k), group)

    def relay_copy(k):
        slot = 2 * near + 2 - k
        return remote(stats_all.at[k, my_part], stats_all.at[slot, my_part],
                      relay_send.at[k], stats_recv.at[slot, 0], partner(2), group)

    def spread_copy(k, j):
        return remote(stats_all.at[k, my_part], stats_all.at[k, my_part],
                      spread_send.at[k, j], stats_recv.at[k, j], me, sibling(j))

    def core_copy(k):
        return remote(stats_all.at[k], stats_all.at[k + 1],
                      core_send.at[k], stats_recv.at[k + 1, 0], partner(1), group)

    own_copy = pltpu.make_async_copy(bins_ref.at[me], bins_all.at[0], own_sem)
    loads = [pltpu.make_async_copy(nodes_ref, labels, load_sem.at[0])]
    for part in range(parts):
        some = pl.ds(part * span, span)
        loads.append(pltpu.make_async_copy(
            grads_ref.at[:, some], stats_all.at[0, part, pl.ds(0, OUT), pl.ds(0, span)],
            load_sem.at[1 + 2 * part]))
        loads.append(pltpu.make_async_copy(
            hess_ref.at[:, some], stats_all.at[0, part, pl.ds(OUT, OUT), pl.ds(0, span)],
            load_sem.at[2 + 2 * part]))
    barrier = pltpu.get_barrier_semaphore()

    def greet(dp, feat):
        pl.semaphore_signal(barrier, inc=1, device_id={"dp": dp, "feat": feat},
                            device_id_type=pl.DeviceIdType.MESH)

    @pl.loop(1, n)
    def _(k):
        greet(partner(k), group)

    @pl.loop(1, parts)
    def _(j):
        greet(me, sibling(j))

    for load in loads:
        load.start()
    own_copy.start()
    pl.semaphore_wait(barrier, n - 1 + parts - 1)

    def each_piece(first, last, act, skip=0):
        @pl.loop(first * steps * halves + skip, last * steps * halves)
        def _(at):
            act(bins_copy(at // (steps * halves), at // halves % steps, at % halves))

    def send(copy):
        copy.start()

    loads[0].wait()
    for part in range(parts):
        for row in range(span // LANES):
            at = part * span + row * LANES
            slot_index = at + lax.broadcasted_iota(jnp.int32, (1, LANES), 1)
            stats_all[0, part, row:row + 1, span:] = jnp.where(
                slot_index < count_ref[0], labels[:, at:at + LANES],
                NODES).astype(jnp.float32)
        stats_all[0, part, span // LANES:, span:] = jnp.zeros(
            (PAIR - span // LANES, LANES), jnp.float32)
    for load in loads[1:]:
        load.wait()

    if line:
        part_copy(near + 2 * middle).start()
        part_copy(2).start()
    else:
        @pl.loop(1, near)
        def _(half):
            part_copy(n - 2 * half).start()

    pair_copy().start()
    each_piece(1, 2, send)

    def send_all(place):
        for k in SEND[place]:
            each_piece(k, k + 1, send)

    if line:
        @pl.when(middle == 0)
        def _():
            send_all(0)

        @pl.when(middle == 1)
        def _():
            each_piece(FIRST, FIRST + 1, send)
    else:
        each_piece(2, n, send)

    left_acc[...] = jnp.zeros_like(left_acc)

    def weigh(k):
        for part in range(parts):
            for row in range(span // LANES):
                block = slice(row * LANES, (row + 1) * LANES)
                stats = stats_all[k, part, :, block]
                label = jnp.broadcast_to(
                    stats_all[k, part, row:row + 1, span:], (PAIR, LANES))
                at = part * span + row * LANES
                for node in range(NODES):
                    weights[k, node * PAIR:(node + 1) * PAIR, at:at + LANES] = jnp.where(
                        label == node, stats, 0.0).astype(jnp.bfloat16)

    def add(k, step, half):
        first = half * (some_feats // width)

        @pl.loop(0, some_feats // width, unroll=min(some_feats // width, 4))
        def _(pair):
            at = first + pair
            total = None
            for start in range(0, cut, ROW_TILE):
                size = min(ROW_TILE, cut - start)
                some = pl.ds(pl.multiple_of(step * cut + start, LANES), size)
                whole = weights[k, :, some]
                levels = lax.broadcasted_iota(jnp.int32, (HIGH, size), 0).astype(jnp.int8)
                above, odd = [], [whole]
                for q in range(width):
                    code = bins_all[k, pl.ds(width * at + q, 1), some]
                    high = (code >> 1).astype(jnp.int8)
                    low = (code & 1).astype(jnp.float32).astype(jnp.bfloat16)
                    above.append(jnp.where(
                        jnp.broadcast_to(high, (HIGH, size)) <= levels,
                        jnp.ones((), MASK), jnp.zeros((), MASK)))
                    odd.append(whole * jnp.broadcast_to(low, (COLS, size)))
                part = lax.dot_general(
                    jnp.concatenate(odd, axis=0), jnp.concatenate(above, axis=0),
                    OVER_LANES, preferred_element_type=jnp.float32)
                total = part if total is None else total + part
            for q in range(width):
                mine = slice(q * HIGH, (q + 1) * HIGH)
                feat = width * at + q
                left_acc[feat, :COLS] = left_acc[feat, :COLS] + total[:COLS, mine]
                left_acc[feat, COLS:] = (
                    left_acc[feat, COLS:] + total[(1 + q) * COLS:(2 + q) * COLS, mine])

    def spread(k):
        @pl.loop(1, parts)
        def _(j):
            spread_copy(k, j).start()

    def gather(k):
        @pl.loop(1, parts)
        def _(j):
            spread_copy(k, j).wait_recv()

        core_copy(k).start()

    lane = lax.broadcasted_iota(jnp.int32, (COLS, HIGH), 1)
    wide = gain_all.shape[-1]
    gain_lane = lax.broadcasted_iota(jnp.int32, (NODES, wide), 1)

    def best_of(feat, gains):
        left_odd, odd = left_acc[feat, :COLS], left_acc[feat, COLS:]
        left_even = left_odd - odd + jnp.where(lane == 0, 0.0, pltpu.roll(odd, 1, axis=1))
        total = left_odd[:, HIGH - 1:]
        whole = jnp.broadcast_to(total, (COLS, HIGH))
        gain = jnp.maximum(two_scores(left_even, whole - left_even),
                           two_scores(left_odd, whole - left_odd))
        best = jnp.max(gain, axis=1, keepdims=True) - score(total)
        return jnp.where(gain_lane == me * own + feat,
                         jnp.broadcast_to(best, (NODES, wide)), gains)

    gain_all[0] = jnp.zeros((NODES, wide), jnp.float32)

    def digits(order):
        return sum(k * n ** at for at, k in enumerate(order))

    @pl.loop(0, n)
    def _(turn):
        k = turn
        if line:
            codes = [digits(order) for order in TAKE]
            code = codes[0] + middle * (codes[1] - codes[0])
            for bit in range(3):
                code = code // (1 + (n ** 2 ** bit - 1) * (turn // 2 ** bit % 2))
            k = code % n

        @pl.when(turn == 0)
        def _():
            own_copy.wait()

        def share(evens):
            for even in evens:
                gather(even)
            for even in evens:
                core_copy(even).wait_recv()

        @pl.when(turn == 1)
        def _():
            if line:
                part_copy(2).wait_recv()
                spread(2)

                @pl.when(middle == 1)
                def _():
                    for even in (near + 2, near):
                        part_copy(even).wait_recv()
                        relay_copy(even).start()
                    send_all(1)
                    spread(near)
                    spread(near + 2)
            else:
                @pl.loop(1, near)
                def _(even):
                    part_copy(2 * even).wait_recv()
                    spread(2 * even)

            pair_copy().wait_recv()

        @pl.when(turn == 2)
        def _():
            share((2,) if line else range(2, n, 2))

        if line:
            @pl.when(jnp.logical_and(turn == 3, middle == 0))
            def _():
                for even in (near, near + 2):
                    part_copy(even).wait_recv()
                    spread(even)

            @pl.when(turn == near)
            def _():
                share((near, near + 2))

        weigh(k)

        @pl.loop(0, steps * halves)
        def _(piece):
            step, half = piece // halves, piece % halves

            @pl.when(k > 0)
            def _():
                bins_copy(k, step, half).wait_recv()

            add(k, step, half)

            @pl.when(jnp.logical_and(turn == n - 1, step == steps - 1))
            def _():
                gain_all[0] = lax.fori_loop(0, some_feats, lambda at, gains: best_of(half * some_feats + at, gains),
                                            gain_all[0], unroll=min(some_feats, 4))

    @pl.loop(1, n)
    def _(k):
        gain_copy(n - k).start()

    @pl.loop(1, n)
    def _(k):
        gain_copy(k).wait_recv()

    out_ref[...] = jnp.sum(gain_all[...], axis=0)[:, :out_ref.shape[1]]

    pair_copy().wait_send()
    if line:
        part_copy(near + 2 * middle).wait_send()
        part_copy(2).wait_send()

        @pl.when(middle == 1)
        def _():
            relay_copy(near).wait_send()
            relay_copy(near + 2).wait_send()

    @pl.loop(1, near)
    def _(half):
        if not line:
            part_copy(2 * half).wait_send()
        core_copy(2 * half).wait_send()

        @pl.loop(1, parts)
        def _(j):
            spread_copy(2 * half, j).wait_send()

    each_piece(1, n, lambda copy: copy.wait_send())

    @pl.loop(1, n)
    def _(k):
        gain_copy(k).wait_send()


def shards(bins, grads, hess, nodes, row_count):
    n = lax.axis_size("dp")
    feats, rows = bins.shape
    own = feats // n
    assert n & (n - 1) == 0 and own * n == feats
    parts = math.gcd(lax.axis_size("feat"), rows // LANES)
    assert n > 7 and parts & (parts - 1) == 0 and rows % (parts * LANES) == 0
    steps = STEPS if rows % (STEPS * LANES) == 0 else 1
    halves = 2 if own % 16 == 0 else 1
    wide = -(-feats // LANES) * LANES
    hbm = pl.BlockSpec(memory_space=pltpu.HBM)
    dma = pltpu.SemaphoreType.DMA
    return pl.pallas_call(
        functools.partial(kernel, n),
        out_shape=jax.ShapeDtypeStruct((NODES, feats), jnp.float32),
        in_specs=[hbm, hbm, hbm, hbm, pl.BlockSpec(memory_space=pltpu.SMEM)],
        out_specs=pl.BlockSpec(memory_space=pltpu.VMEM),
        scratch_shapes=[
            pltpu.VMEM((n, own, rows), jnp.int32),
            pltpu.VMEM((n, parts, PAIR, rows // parts + LANES), jnp.float32),
            pltpu.VMEM((n, COLS, rows), jnp.bfloat16),
            pltpu.VMEM((own, 2 * COLS, HIGH), jnp.float32),
            pltpu.VMEM((n, NODES, wide), jnp.float32),
            pltpu.VMEM((1, rows), jnp.int32),
            dma, dma((1 + 2 * parts,)), dma((n, steps, halves)), dma((n, steps, halves)),
            dma((n,)), dma((n, parts)), dma((n,)), dma((n,)), dma((n, parts)),
            dma((n,)), dma((n,)),
        ],
        compiler_params=pltpu.CompilerParams(
            collective_id=0, has_side_effects=True, vmem_limit_bytes=(64 << 20) - 8192),
        name="histogram_gain",
    )(bins.reshape(n, own, rows), grads, hess, nodes.reshape(1, rows), row_count)


def solution(mesh):
    in_specs = (P("feat", "dp"), P(None, "dp"), P(None, "dp"), P("dp"), P("dp"))
    out_specs = P(None, "feat")
    return jax.shard_map(shards, mesh=mesh, in_specs=in_specs, out_specs=out_specs, check_vma=False)
```

```python
import functools
import math

import jax
import jax.numpy as jnp
from jax import lax
from jax.experimental import pallas as pl
from jax.experimental.pallas import tpu as pltpu
from jax.sharding import PartitionSpec as P

BINS = 256
OUT = 8
NODES = 4
PAIR = 2 * OUT
COLS = NODES * PAIR
HIGH = BINS // 2
LANES = 128
ROW_TILE = 512
STEPS = 1
SEND = ((2, 3, 4, 5, 6, 7), (2, 3, 7, 4, 5))
FIRST = 6
TAKE = ((0, 1, 2, 3, 6, 7, 4, 5), (0, 1, 2, 3, 6, 7, 4, 5))
OVER_LANES = (((1,), (1,)), ((), ()))
MASK = jnp.float8_e4m3fn


def columns(sums):
    shaped = sums.reshape(NODES, PAIR, sums.shape[-1])
    return shaped[:, :OUT, :], shaped[:, OUT:, :] + 1.0


def score(sums):
    grad_sum, hess_sum = columns(sums)
    return jnp.sum(grad_sum * grad_sum / hess_sum, axis=1)


def two_scores(left, right):
    left_grad, left_hess = columns(left)
    right_grad, right_hess = columns(right)
    top = left_grad * left_grad * right_hess + right_grad * right_grad * left_hess
    return jnp.sum(top / (left_hess * right_hess), axis=1)


def flip(index, k, size):
    other, bit = 0, 1
    while bit < size:
        other = other + ((index // bit + k // bit) % 2) * bit
        bit *= 2
    return other


def kernel(n, bins_ref, grads_ref, hess_ref, nodes_ref, count_ref, out_ref,
           bins_all, stats_all, weights, left_acc, gain_all, labels,
           own_sem, load_sem, bins_send, bins_recv, direct_send, spread_send, core_send, relay_send, stats_recv,
           gain_send, gain_recv):
    own, rows = bins_all.shape[1:]
    parts = stats_all.shape[1]
    span = rows // parts
    steps, halves = bins_send.shape[1:]
    cut, some_feats = rows // steps, own // halves
    line = n == 8
    near = n // 2
    width = 2 if own % 2 == 0 else 1
    me = lax.axis_index("dp")
    group = lax.axis_index("feat")
    my_part = group % parts
    middle = (me // 2 + me // 4) % 2

    def partner(k):
        return flip(me, k, n)

    def sibling(j):
        return group - my_part + flip(my_part, j, parts)

    def remote(src, dst, send, recv, dp, feat):
        return pltpu.make_async_remote_copy(
            src_ref=src, dst_ref=dst, send_sem=send, recv_sem=recv,
            device_id={"dp": dp, "feat": feat}, device_id_type=pl.DeviceIdType.MESH)

    def bins_copy(k, step, half):
        some = (pl.ds(half * some_feats, some_feats), pl.ds(pl.multiple_of(step * cut, LANES), cut))
        return remote(bins_ref.at[partner(k), *some], bins_all.at[k, *some],
                      bins_send.at[k, step, half], bins_recv.at[k, step, half], partner(k), group)

    def gain_copy(k):
        return remote(gain_all.at[0], gain_all.at[k],
                      gain_send.at[k], gain_recv.at[k], partner(k), group)

    def pair_copy():
        return remote(stats_all.at[0], stats_all.at[1],
                      direct_send.at[1], stats_recv.at[1, 0], partner(1), group)

    def part_copy(k):
        return remote(stats_all.at[0, my_part], stats_all.at[k, my_part],
                      direct_send.at[k], stats_recv.at[k, 0], partner(k), group)

    def relay_copy(k):
        slot = 2 * near + 2 - k
        return remote(stats_all.at[k, my_part], stats_all.at[slot, my_part],
                      relay_send.at[k], stats_recv.at[slot, 0], partner(2), group)

    def spread_copy(k, j):
        return remote(stats_all.at[k, my_part], stats_all.at[k, my_part],
                      spread_send.at[k, j], stats_recv.at[k, j], me, sibling(j))

    def core_copy(k):
        return remote(stats_all.at[k], stats_all.at[k + 1],
                      core_send.at[k], stats_recv.at[k + 1, 0], partner(1), group)

    own_copy = pltpu.make_async_copy(bins_ref.at[me], bins_all.at[0], own_sem)
    loads = [pltpu.make_async_copy(nodes_ref, labels, load_sem.at[0])]
    for part in range(parts):
        some = pl.ds(part * span, span)
        loads.append(pltpu.make_async_copy(
            grads_ref.at[:, some], stats_all.at[0, part, pl.ds(0, OUT), pl.ds(0, span)],
            load_sem.at[1 + 2 * part]))
        loads.append(pltpu.make_async_copy(
            hess_ref.at[:, some], stats_all.at[0, part, pl.ds(OUT, OUT), pl.ds(0, span)],
            load_sem.at[2 + 2 * part]))
    barrier = pltpu.get_barrier_semaphore()

    def greet(dp, feat):
        pl.semaphore_signal(barrier, inc=1, device_id={"dp": dp, "feat": feat},
                            device_id_type=pl.DeviceIdType.MESH)

    @pl.loop(1, n)
    def _(k):
        greet(partner(k), group)

    @pl.loop(1, parts)
    def _(j):
        greet(me, sibling(j))

    for load in loads:
        load.start()
    own_copy.start()
    pl.semaphore_wait(barrier, n - 1 + parts - 1)

    def each_piece(first, last, act, skip=0):
        @pl.loop(first * steps * halves + skip, last * steps * halves)
        def _(at):
            act(bins_copy(at // (steps * halves), at // halves % steps, at % halves))

    def send(copy):
        copy.start()

    loads[0].wait()
    for part in range(parts):
        for row in range(span // LANES):
            at = part * span + row * LANES
            slot_index = at + lax.broadcasted_iota(jnp.int32, (1, LANES), 1)
            stats_all[0, part, row:row + 1, span:] = jnp.where(
                slot_index < count_ref[0], labels[:, at:at + LANES],
                NODES).astype(jnp.float32)
        stats_all[0, part, span // LANES:, span:] = jnp.zeros(
            (PAIR - span // LANES, LANES), jnp.float32)
    for load in loads[1:]:
        load.wait()

    if line:
        part_copy(near + 2 * middle).start()
        part_copy(2).start()
    else:
        @pl.loop(1, near)
        def _(half):
            part_copy(n - 2 * half).start()

    pair_copy().start()
    each_piece(1, 2, send)

    def send_all(place):
        for k in SEND[place]:
            each_piece(k, k + 1, send)

    if line:
        @pl.when(middle == 0)
        def _():
            send_all(0)

        @pl.when(middle == 1)
        def _():
            each_piece(FIRST, FIRST + 1, send)
    else:
        each_piece(2, n, send)

    left_acc[...] = jnp.zeros_like(left_acc)

    def weigh(k):
        for part in range(parts):
            for row in range(span // LANES):
                block = slice(row * LANES, (row + 1) * LANES)
                stats = stats_all[k, part, :, block]
                label = jnp.broadcast_to(
                    stats_all[k, part, row:row + 1, span:], (PAIR, LANES))
                at = part * span + row * LANES
                for node in range(NODES):
                    weights[k, node * PAIR:(node + 1) * PAIR, at:at + LANES] = jnp.where(
                        label == node, stats, 0.0).astype(jnp.bfloat16)

    def add(k, step, half):
        first = half * (some_feats // width)

        @pl.loop(0, some_feats // width, unroll=min(some_feats // width, 4))
        def _(pair):
            at = first + pair
            total = None
            for start in range(0, cut, ROW_TILE):
                size = min(ROW_TILE, cut - start)
                some = pl.ds(pl.multiple_of(step * cut + start, LANES), size)
                whole = weights[k, :, some]
                levels = lax.broadcasted_iota(jnp.int32, (HIGH, size), 0).astype(jnp.int8)
                above, odd = [], [whole]
                for q in range(width):
                    code = bins_all[k, pl.ds(width * at + q, 1), some]
                    high = (code >> 1).astype(jnp.int8)
                    low = (code & 1).astype(jnp.float32).astype(jnp.bfloat16)
                    above.append(jnp.where(
                        jnp.broadcast_to(high, (HIGH, size)) <= levels,
                        jnp.ones((), MASK), jnp.zeros((), MASK)))
                    odd.append(whole * jnp.broadcast_to(low, (COLS, size)))
                part = lax.dot_general(
                    jnp.concatenate(odd, axis=0), jnp.concatenate(above, axis=0),
                    OVER_LANES, preferred_element_type=jnp.float32)
                total = part if total is None else total + part
            for q in range(width):
                mine = slice(q * HIGH, (q + 1) * HIGH)
                feat = width * at + q
                left_acc[feat, :COLS] = left_acc[feat, :COLS] + total[:COLS, mine]
                left_acc[feat, COLS:] = (
                    left_acc[feat, COLS:] + total[(1 + q) * COLS:(2 + q) * COLS, mine])

    def spread(k):
        @pl.loop(1, parts)
        def _(j):
            spread_copy(k, j).start()

    def gather(k):
        @pl.loop(1, parts)
        def _(j):
            spread_copy(k, j).wait_recv()

        core_copy(k).start()

    lane = lax.broadcasted_iota(jnp.int32, (COLS, HIGH), 1)
    wide = gain_all.shape[-1]
    gain_lane = lax.broadcasted_iota(jnp.int32, (NODES, wide), 1)

    def best_of(feat, gains):
        left_odd, odd = left_acc[feat, :COLS], left_acc[feat, COLS:]
        left_even = left_odd - odd + jnp.where(lane == 0, 0.0, pltpu.roll(odd, 1, axis=1))
        total = left_odd[:, HIGH - 1:]
        whole = jnp.broadcast_to(total, (COLS, HIGH))
        gain = jnp.maximum(two_scores(left_even, whole - left_even),
                           two_scores(left_odd, whole - left_odd))
        best = jnp.max(gain, axis=1, keepdims=True) - score(total)
        return jnp.where(gain_lane == me * own + feat,
                         jnp.broadcast_to(best, (NODES, wide)), gains)

    gain_all[0] = jnp.zeros((NODES, wide), jnp.float32)

    def digits(order):
        return sum(k * n ** at for at, k in enumerate(order))

    @pl.loop(0, n)
    def _(turn):
        k = turn
        if line:
            codes = [digits(order) for order in TAKE]
            code = codes[0] + middle * (codes[1] - codes[0])
            for bit in range(3):
                code = code // (1 + (n ** 2 ** bit - 1) * (turn // 2 ** bit % 2))
            k = code % n

        @pl.when(turn == 0)
        def _():
            own_copy.wait()

        def share(evens):
            for even in evens:
                gather(even)
            for even in evens:
                core_copy(even).wait_recv()

        @pl.when(turn == 1)
        def _():
            if line:
                part_copy(2).wait_recv()
                spread(2)

                @pl.when(middle == 1)
                def _():
                    for even in (near + 2, near):
                        part_copy(even).wait_recv()
                        relay_copy(even).start()
                    send_all(1)
                    spread(near)
                    spread(near + 2)
            else:
                @pl.loop(1, near)
                def _(even):
                    part_copy(2 * even).wait_recv()
                    spread(2 * even)

            pair_copy().wait_recv()

        @pl.when(turn == 2)
        def _():
            share((2,) if line else range(2, n, 2))

        if line:
            @pl.when(jnp.logical_and(turn == 3, middle == 0))
            def _():
                for even in (near, near + 2):
                    part_copy(even).wait_recv()
                    spread(even)

            @pl.when(turn == near)
            def _():
                share((near, near + 2))

        weigh(k)

        @pl.loop(0, steps * halves)
        def _(piece):
            step, half = piece // halves, piece % halves

            @pl.when(k > 0)
            def _():
                bins_copy(k, step, half).wait_recv()

            add(k, step, half)

            @pl.when(jnp.logical_and(turn == n - 1, step == steps - 1))
            def _():
                gain_all[0] = lax.fori_loop(0, some_feats, lambda at, gains: best_of(half * some_feats + at, gains),
                                            gain_all[0], unroll=min(some_feats, 4))

    @pl.loop(1, n)
    def _(k):
        gain_copy(n - k).start()

    @pl.loop(1, n)
    def _(k):
        gain_copy(k).wait_recv()

    out_ref[...] = jnp.sum(gain_all[...], axis=0)[:, :out_ref.shape[1]]

    pair_copy().wait_send()
    if line:
        part_copy(near + 2 * middle).wait_send()
        part_copy(2).wait_send()

        @pl.when(middle == 1)
        def _():
            relay_copy(near).wait_send()
            relay_copy(near + 2).wait_send()

    @pl.loop(1, near)
    def _(half):
        if not line:
            part_copy(2 * half).wait_send()
        core_copy(2 * half).wait_send()

        @pl.loop(1, parts)
        def _(j):
            spread_copy(2 * half, j).wait_send()

    each_piece(1, n, lambda copy: copy.wait_send())

    @pl.loop(1, n)
    def _(k):
        gain_copy(k).wait_send()


def shards(bins, grads, hess, nodes, row_count):
    n = lax.axis_size("dp")
    feats, rows = bins.shape
    own = feats // n
    assert n & (n - 1) == 0 and own * n == feats
    parts = math.gcd(lax.axis_size("feat"), rows // LANES)
    assert n > 7 and parts & (parts - 1) == 0 and rows % (parts * LANES) == 0
    steps = STEPS if rows % (STEPS * LANES) == 0 else 1
    halves = 4 if own % 16 == 0 else 1
    wide = -(-feats // LANES) * LANES
    hbm = pl.BlockSpec(memory_space=pltpu.HBM)
    dma = pltpu.SemaphoreType.DMA
    return pl.pallas_call(
        functools.partial(kernel, n),
        out_shape=jax.ShapeDtypeStruct((NODES, feats), jnp.float32),
        in_specs=[hbm, hbm, hbm, hbm, pl.BlockSpec(memory_space=pltpu.SMEM)],
        out_specs=pl.BlockSpec(memory_space=pltpu.VMEM),
        scratch_shapes=[
            pltpu.VMEM((n, own, rows), jnp.int32),
            pltpu.VMEM((n, parts, PAIR, rows // parts + LANES), jnp.float32),
            pltpu.VMEM((n, COLS, rows), jnp.bfloat16),
            pltpu.VMEM((own, 2 * COLS, HIGH), jnp.float32),
            pltpu.VMEM((n, NODES, wide), jnp.float32),
            pltpu.VMEM((1, rows), jnp.int32),
            dma, dma((1 + 2 * parts,)), dma((n, steps, halves)), dma((n, steps, halves)),
            dma((n,)), dma((n, parts)), dma((n,)), dma((n,)), dma((n, parts)),
            dma((n,)), dma((n,)),
        ],
        compiler_params=pltpu.CompilerParams(
            collective_id=0, has_side_effects=True, vmem_limit_bytes=(64 << 20) - 8192),
        name="histogram_gain",
    )(bins.reshape(n, own, rows), grads, hess, nodes.reshape(1, rows), row_count)


def solution(mesh):
    in_specs = (P("feat", "dp"), P(None, "dp"), P(None, "dp"), P("dp"), P("dp"))
    out_specs = P(None, "feat")
    return jax.shard_map(shards, mesh=mesh, in_specs=in_specs, out_specs=out_specs, check_vma=False)
```

```python
import functools
import math

import jax
import jax.numpy as jnp
from jax import lax
from jax.experimental import pallas as pl
from jax.experimental.pallas import tpu as pltpu
from jax.sharding import PartitionSpec as P

BINS = 256
OUT = 8
NODES = 4
PAIR = 2 * OUT
COLS = NODES * PAIR
HIGH = BINS // 2
LANES = 128
ROW_TILE = 512
STEPS = 1
SEND = ((2, 3, 4, 5, 6, 7), (2, 3, 7, 4, 5))
FIRST = 6
TAKE = ((0, 1, 2, 3, 6, 7, 4, 5), (0, 1, 2, 3, 6, 7, 4, 5))
OVER_LANES = (((1,), (1,)), ((), ()))
MASK = jnp.float8_e4m3fn


def columns(sums):
    shaped = sums.reshape(NODES, PAIR, sums.shape[-1])
    return shaped[:, :OUT, :], shaped[:, OUT:, :] + 1.0


def score(sums):
    grad_sum, hess_sum = columns(sums)
    return jnp.sum(grad_sum * grad_sum / hess_sum, axis=1)


def two_scores(left, right):
    left_grad, left_hess = columns(left)
    right_grad, right_hess = columns(right)
    top = left_grad * left_grad * right_hess + right_grad * right_grad * left_hess
    return jnp.sum(top / (left_hess * right_hess), axis=1)


def flip(index, k, size):
    other, bit = 0, 1
    while bit < size:
        other = other + ((index // bit + k // bit) % 2) * bit
        bit *= 2
    return other


def kernel(n, bins_ref, grads_ref, hess_ref, nodes_ref, count_ref, out_ref,
           bins_all, stats_all, weights, left_acc, gain_all, labels,
           own_sem, load_sem, bins_send, bins_recv, direct_send, spread_send, core_send, relay_send, stats_recv,
           gain_send, gain_recv):
    own, rows = bins_all.shape[1:]
    parts = stats_all.shape[1]
    span = rows // parts
    steps, halves = bins_send.shape[1:]
    cut, some_feats = rows // steps, own // halves
    line = n == 8
    near = n // 2
    width = 2 if own % 2 == 0 else 1
    me = lax.axis_index("dp")
    group = lax.axis_index("feat")
    my_part = group % parts
    middle = (me // 2 + me // 4) % 2

    def partner(k):
        return flip(me, k, n)

    def sibling(j):
        return group - my_part + flip(my_part, j, parts)

    def remote(src, dst, send, recv, dp, feat):
        return pltpu.make_async_remote_copy(
            src_ref=src, dst_ref=dst, send_sem=send, recv_sem=recv,
            device_id={"dp": dp, "feat": feat}, device_id_type=pl.DeviceIdType.MESH)

    def bins_copy(k, step, half):
        some = (pl.ds(half * some_feats, some_feats), pl.ds(pl.multiple_of(step * cut, LANES), cut))
        return remote(bins_ref.at[partner(k), *some], bins_all.at[k, *some],
                      bins_send.at[k, step, half], bins_recv.at[k, step, half], partner(k), group)

    def gain_copy(k):
        return remote(gain_all.at[0], gain_all.at[k],
                      gain_send.at[k], gain_recv.at[k], partner(k), group)

    def pair_copy():
        return remote(stats_all.at[0], stats_all.at[1],
                      direct_send.at[1], stats_recv.at[1, 0], partner(1), group)

    def part_copy(k):
        return remote(stats_all.at[0, my_part], stats_all.at[k, my_part],
                      direct_send.at[k], stats_recv.at[k, 0], partner(k), group)

    def relay_copy(k):
        slot = 2 * near + 2 - k
        return remote(stats_all.at[k, my_part], stats_all.at[slot, my_part],
                      relay_send.at[k], stats_recv.at[slot, 0], partner(2), group)

    def spread_copy(k, j):
        return remote(stats_all.at[k, my_part], stats_all.at[k, my_part],
                      spread_send.at[k, j], stats_recv.at[k, j], me, sibling(j))

    def core_copy(k):
        return remote(stats_all.at[k], stats_all.at[k + 1],
                      core_send.at[k], stats_recv.at[k + 1, 0], partner(1), group)

    own_copy = pltpu.make_async_copy(bins_ref.at[me], bins_all.at[0], own_sem)
    loads = [pltpu.make_async_copy(nodes_ref, labels, load_sem.at[0])]
    for part in range(parts):
        some = pl.ds(part * span, span)
        loads.append(pltpu.make_async_copy(
            grads_ref.at[:, some], stats_all.at[0, part, pl.ds(0, OUT), pl.ds(0, span)],
            load_sem.at[1 + 2 * part]))
        loads.append(pltpu.make_async_copy(
            hess_ref.at[:, some], stats_all.at[0, part, pl.ds(OUT, OUT), pl.ds(0, span)],
            load_sem.at[2 + 2 * part]))
    barrier = pltpu.get_barrier_semaphore()

    def greet(dp, feat):
        pl.semaphore_signal(barrier, inc=1, device_id={"dp": dp, "feat": feat},
                            device_id_type=pl.DeviceIdType.MESH)

    @pl.loop(1, n)
    def _(k):
        greet(partner(k), group)

    @pl.loop(1, parts)
    def _(j):
        greet(me, sibling(j))

    for load in loads:
        load.start()
    own_copy.start()
    pl.semaphore_wait(barrier, n - 1 + parts - 1)

    def each_piece(first, last, act, skip=0):
        @pl.loop(first * steps * halves + skip, last * steps * halves)
        def _(at):
            act(bins_copy(at // (steps * halves), at // halves % steps, at % halves))

    def send(copy):
        copy.start()

    loads[0].wait()
    for part in range(parts):
        for row in range(span // LANES):
            at = part * span + row * LANES
            slot_index = at + lax.broadcasted_iota(jnp.int32, (1, LANES), 1)
            stats_all[0, part, row:row + 1, span:] = jnp.where(
                slot_index < count_ref[0], labels[:, at:at + LANES],
                NODES).astype(jnp.float32)
        stats_all[0, part, span // LANES:, span:] = jnp.zeros(
            (PAIR - span // LANES, LANES), jnp.float32)
    for load in loads[1:]:
        load.wait()

    if line:
        part_copy(near + 2 * middle).start()
        part_copy(2).start()
    else:
        @pl.loop(1, near)
        def _(half):
            part_copy(n - 2 * half).start()

    pair_copy().start()
    each_piece(1, 2, send)

    def send_all(place):
        for k in SEND[place]:
            each_piece(k, k + 1, send)

    if line:
        @pl.when(middle == 0)
        def _():
            send_all(0)

        @pl.when(middle == 1)
        def _():
            each_piece(FIRST, FIRST + 1, send)
    else:
        each_piece(2, n, send)

    left_acc[...] = jnp.zeros_like(left_acc)

    def weigh(k):
        for part in range(parts):
            for row in range(span // LANES):
                block = slice(row * LANES, (row + 1) * LANES)
                stats = stats_all[k, part, :, block]
                label = jnp.broadcast_to(
                    stats_all[k, part, row:row + 1, span:], (PAIR, LANES))
                at = part * span + row * LANES
                for node in range(NODES):
                    weights[k, node * PAIR:(node + 1) * PAIR, at:at + LANES] = jnp.where(
                        label == node, stats, 0.0).astype(jnp.bfloat16)

    def add(k, step, half):
        first = half * (some_feats // width)

        @pl.loop(0, some_feats // width, unroll=min(some_feats // width, 4))
        def _(pair):
            at = first + pair
            total = None
            for start in range(0, cut, ROW_TILE):
                size = min(ROW_TILE, cut - start)
                some = pl.ds(pl.multiple_of(step * cut + start, LANES), size)
                whole = weights[k, :, some]
                levels = lax.broadcasted_iota(jnp.int32, (HIGH, size), 0).astype(jnp.int8)
                above, odd = [], [whole]
                for q in range(width):
                    code = bins_all[k, pl.ds(width * at + q, 1), some]
                    high = (code >> 1).astype(jnp.int8)
                    low = (code & 1).astype(jnp.float32).astype(jnp.bfloat16)
                    above.append(jnp.where(
                        jnp.broadcast_to(high, (HIGH, size)) <= levels,
                        jnp.ones((), MASK), jnp.zeros((), MASK)))
                    odd.append(whole * jnp.broadcast_to(low, (COLS, size)))
                part = lax.dot_general(
                    jnp.concatenate(odd, axis=0), jnp.concatenate(above, axis=0),
                    OVER_LANES, preferred_element_type=jnp.float32)
                total = part if total is None else total + part
            for q in range(width):
                mine = slice(q * HIGH, (q + 1) * HIGH)
                feat = width * at + q
                left_acc[feat, :COLS] = left_acc[feat, :COLS] + total[:COLS, mine]
                left_acc[feat, COLS:] = (
                    left_acc[feat, COLS:] + total[(1 + q) * COLS:(2 + q) * COLS, mine])

    def spread(k):
        @pl.loop(1, parts)
        def _(j):
            spread_copy(k, j).start()

    def gather(k):
        @pl.loop(1, parts)
        def _(j):
            spread_copy(k, j).wait_recv()

        core_copy(k).start()

    lane = lax.broadcasted_iota(jnp.int32, (COLS, HIGH), 1)
    wide = gain_all.shape[-1]
    gain_lane = lax.broadcasted_iota(jnp.int32, (NODES, wide), 1)

    def best_of(feat, gains):
        left_odd, odd = left_acc[feat, :COLS], left_acc[feat, COLS:]
        left_even = left_odd - odd + jnp.where(lane == 0, 0.0, pltpu.roll(odd, 1, axis=1))
        total = left_odd[:, HIGH - 1:]
        whole = jnp.broadcast_to(total, (COLS, HIGH))
        gain = jnp.maximum(two_scores(left_even, whole - left_even),
                           two_scores(left_odd, whole - left_odd))
        best = jnp.max(gain, axis=1, keepdims=True) - score(total)
        return jnp.where(gain_lane == me * own + feat,
                         jnp.broadcast_to(best, (NODES, wide)), gains)

    gain_all[0] = jnp.zeros((NODES, wide), jnp.float32)

    def digits(order):
        return sum(k * n ** at for at, k in enumerate(order))

    @pl.loop(0, n)
    def _(turn):
        k = turn
        if line:
            codes = [digits(order) for order in TAKE]
            code = codes[0] + middle * (codes[1] - codes[0])
            for bit in range(3):
                code = code // (1 + (n ** 2 ** bit - 1) * (turn // 2 ** bit % 2))
            k = code % n

        @pl.when(turn == 0)
        def _():
            own_copy.wait()

        def share(evens):
            for even in evens:
                gather(even)
            for even in evens:
                core_copy(even).wait_recv()

        @pl.when(turn == 1)
        def _():
            if line:
                part_copy(2).wait_recv()
                spread(2)

                @pl.when(middle == 1)
                def _():
                    for even in (near + 2, near):
                        part_copy(even).wait_recv()
                        relay_copy(even).start()
                    send_all(1)
                    spread(near)
                    spread(near + 2)
            else:
                @pl.loop(1, near)
                def _(even):
                    part_copy(2 * even).wait_recv()
                    spread(2 * even)

            pair_copy().wait_recv()

        @pl.when(turn == 2)
        def _():
            share((2,) if line else range(2, n, 2))

        if line:
            @pl.when(jnp.logical_and(turn == 3, middle == 0))
            def _():
                for even in (near, near + 2):
                    part_copy(even).wait_recv()
                    spread(even)

            @pl.when(turn == near)
            def _():
                share((near, near + 2))

        weigh(k)

        @pl.loop(0, steps * halves)
        def _(piece):
            step, half = piece // halves, piece % halves

            @pl.when(k > 0)
            def _():
                bins_copy(k, step, half).wait_recv()

            add(k, step, half)

            @pl.when(jnp.logical_and(turn == n - 1, step == steps - 1))
            def _():
                gain_all[0] = lax.fori_loop(0, some_feats, lambda at, gains: best_of(half * some_feats + at, gains),
                                            gain_all[0], unroll=min(some_feats, 4))

    @pl.loop(1, n)
    def _(k):
        gain_copy(n - k).start()

    pair_copy().wait_send()
    if line:
        part_copy(near + 2 * middle).wait_send()
        part_copy(2).wait_send()

        @pl.when(middle == 1)
        def _():
            relay_copy(near).wait_send()
            relay_copy(near + 2).wait_send()

    @pl.loop(1, near)
    def _(half):
        if not line:
            part_copy(2 * half).wait_send()
        core_copy(2 * half).wait_send()

        @pl.loop(1, parts)
        def _(j):
            spread_copy(2 * half, j).wait_send()

    each_piece(1, n, lambda copy: copy.wait_send())

    @pl.loop(1, n)
    def _(k):
        gain_copy(k).wait_recv()

    out_ref[...] = jnp.sum(gain_all[...], axis=0)[:, :out_ref.shape[1]]

    @pl.loop(1, n)
    def _(k):
        gain_copy(k).wait_send()


def shards(bins, grads, hess, nodes, row_count):
    n = lax.axis_size("dp")
    feats, rows = bins.shape
    own = feats // n
    assert n & (n - 1) == 0 and own * n == feats
    parts = math.gcd(lax.axis_size("feat"), rows // LANES)
    assert n > 7 and parts & (parts - 1) == 0 and rows % (parts * LANES) == 0
    steps = STEPS if rows % (STEPS * LANES) == 0 else 1
    halves = 2 if own % 16 == 0 else 1
    wide = -(-feats // LANES) * LANES
    hbm = pl.BlockSpec(memory_space=pltpu.HBM)
    dma = pltpu.SemaphoreType.DMA
    return pl.pallas_call(
        functools.partial(kernel, n),
        out_shape=jax.ShapeDtypeStruct((NODES, feats), jnp.float32),
        in_specs=[hbm, hbm, hbm, hbm, pl.BlockSpec(memory_space=pltpu.SMEM)],
        out_specs=pl.BlockSpec(memory_space=pltpu.VMEM),
        scratch_shapes=[
            pltpu.VMEM((n, own, rows), jnp.int32),
            pltpu.VMEM((n, parts, PAIR, rows // parts + LANES), jnp.float32),
            pltpu.VMEM((n, COLS, rows), jnp.bfloat16),
            pltpu.VMEM((own, 2 * COLS, HIGH), jnp.float32),
            pltpu.VMEM((n, NODES, wide), jnp.float32),
            pltpu.VMEM((1, rows), jnp.int32),
            dma, dma((1 + 2 * parts,)), dma((n, steps, halves)), dma((n, steps, halves)),
            dma((n,)), dma((n, parts)), dma((n,)), dma((n,)), dma((n, parts)),
            dma((n,)), dma((n,)),
        ],
        compiler_params=pltpu.CompilerParams(
            collective_id=0, has_side_effects=True, vmem_limit_bytes=(64 << 20) - 8192),
        name="histogram_gain",
    )(bins.reshape(n, own, rows), grads, hess, nodes.reshape(1, rows), row_count)


def solution(mesh):
    in_specs = (P("feat", "dp"), P(None, "dp"), P(None, "dp"), P("dp"), P("dp"))
    out_specs = P(None, "feat")
    return jax.shard_map(shards, mesh=mesh, in_specs=in_specs, out_specs=out_specs, check_vma=False)
```
